256 devices in a mesh: seq: 64 (over z, y, core), batch: 4 (over x).
Axes of the slice: x: 4, y: 4, z: 8, core: 2. Of those that a mesh axis runs over, the one named last changes fastest.
Arguments:
- tokens: bfloat16 [32768, 1440], P(('batch', 'seq')), parts along dimension 0, may hold values from -6 to 6
- norm_gain: float32 [1440], replicated, may hold values from 0.1 to 1.9
- qkv_weight: bfloat16 [1440, 2560], P(None, 'seq'), may hold values from -2 to 2
- sinks: float32 [32], replicated, may hold values from 0 to 5
- out_weight: bfloat16 [2048, 1440], P('seq'), may hold values from -0.125 to 0.125
- moe_gain: float32 [1440], replicated, may hold values from 0.1 to 1.9
- expert_in: bfloat16 [64, 1440, 2880], P('seq'), may hold values from -0.15625 to 0.15625
- expert_out: bfloat16 [64, 1440, 1440], P('seq'), may hold values from -0.15625 to 0.15625
- expert_ids: int32 [32768, 4], P(('batch', 'seq')), parts along dimension 0, may hold values from 0 to 63, all different within a row; in each aligned block of 128 rows (0 to 127, 128 to 255, ...) at most 16 rows name the same one
- gate_ints: int32 [32768, 4], P(('batch', 'seq')), parts along dimension 0, may hold values from 1 to 4096
Outputs:
- block_out: bfloat16 [32768, 1440], P(('batch', 'seq')), parts along dimension 0
The draws below stay inside these ranges and needn't reach their ends.
There are 4 independent parts, one for each index of `batch`. The reference program is written for one: setup_inputs(seed, part) draws one part's arguments, and reference() takes and returns one part's arrays. A program takes and returns all parts, laid end to end along the dimension named above; an argument that names none is the same for every part. Nothing has to cross between parts.
Inputs may be any that keep to these rules, and one draw needn't show every extreme that they name: `expert_ids`: each row names 4 different experts; among the 128 rows of one device no expert is named more than 16 times.
All inputs are finite; a program needn't handle non-finite values.
Results may differ from the reference program's by a relative error of at most 0.012.
Values may be sent and summed in bfloat16 or wider, within the bound.
No kernel may reach another device: no remote copies, remote signals or barrier semaphores. Data moves between devices by JAX's collectives and lax.ppermute only.
A program may use at most 128 MiB of HBM per device.

```python
import math
import jax
import jax.numpy as jnp
import numpy as np
from jax import lax

D = 1440
H = 1440
QH = 32
KVH = 4
HD = 64
WIN = 128
TOP = 4
TOK_DEV = 128
EXPERTS = 64
CAP = 16
SEQ_LEN = 8192
N_SEQ = 64


def draw_qkv_weight(key, part):
    columns = (QH + 2 * KVH) * HD
    normal_part = jax.random.truncated_normal(key, -4.0, 4.0, (D, columns), jnp.float32) * D ** (-0.5)
    return jnp.clip(normal_part, -2.0, 2.0).astype(jnp.bfloat16)


def place_ends(array, stream_key, least, top_value):
    longest = array.shape.index(max(array.shape))
    spots = []
    for shift in (0, 1):
        where = [jax.random.randint(jax.random.fold_in(stream_key, axis), (), 0, length) for axis, length in enumerate(array.shape)]
        where[longest] = (where[longest] + shift) % array.shape[longest]
        spots.append(tuple(where))
    return array.at[spots[0]].set(least).at[spots[1]].set(top_value)


def block_levels(key, shape, shards, least, top_value):
    factor_of = 1.0
    for position, parts in shards:
        steps = jax.random.uniform(jax.random.fold_in(jax.random.fold_in(key, 6), position), (parts,), jnp.float32, least / len(shards), top_value / len(shards))
        factor_of = factor_of * jnp.repeat(jnp.exp(steps), shape[position] // parts).reshape((-1,) + (1,) * (len(shape) - 1 - position))
    return factor_of


def routed_block(own_key, own, number, rows, count, top, most, lean):
    order = jax.random.permutation(own_key, count)
    packed, usual = load_shares(count, rows * top, most, lean, True), load_shares(count, rows * top, most, lean, False)
    places = jnp.arange(count)

    def named(tallies, offset_by):
        used = int((tallies > 0).sum())
        fixed = max(1, used // 4)
        shifted = fixed + (places - fixed + offset_by * (used - fixed)) % max(1, count - fixed)
        return jnp.zeros((count,), jnp.int32).at[order[jnp.where(places < fixed, places, shifted)]].set(jnp.asarray(tallies, jnp.int32))

    tallies = jnp.where(number % 4 == 0, named(packed, number // 4), named(usual, number - number // 4 - 1))
    mixed = jax.random.permutation(jax.random.fold_in(own, 3), count)
    source_of, sink = mixed[0:count // 2 * 2:2], mixed[1:count // 2 * 2:2]
    slack = jnp.minimum(tallies[source_of] - 1, most - tallies[sink]) // 2
    slack = jnp.where((source_of == order[0]) | (sink == order[0]) | (tallies[sink] == 0), 0, jnp.maximum(slack, 0))
    shifted = jax.random.randint(jax.random.fold_in(own, 4), (count // 2,), 0, 1 << 20) % (slack + 1)
    tallies = tallies.at[source_of].add(-shifted).at[sink].add(shifted)
    members = jnp.searchsorted(jnp.cumsum(tallies), jnp.arange(rows * top), side="right").astype(jnp.int32)
    listing = members.reshape(top, rows).T
    listing = listing[jax.random.permutation(jax.random.fold_in(own, 1), rows)]
    offset_by = jax.random.randint(jax.random.fold_in(own, 2), (rows, 1), 0, top)
    return jnp.take_along_axis(listing, (jnp.arange(top)[None, :] + offset_by) % top, axis=1)


def load_shares(count, total, most, slope, full):
    loads = [(1 << 20) // math.isqrt(grade ** slope) + 1 for grade in range(1, count + 1)]
    largest = most if full else min(most, max(-(-total // count), total * loads[0] // sum(loads)))
    least = 1 if total - largest >= count - 1 else 0
    given, spare = [largest] + [least] * (count - 1), total - largest - least * (count - 1)
    while spare > 0:
        movable = [i for i in range(1, count) if given[i] < largest] or [i for i in range(1, count) if given[i] < most]
        mass, budget = sum([loads[i] for i in movable]), spare
        for i in movable:
            extra = min(most - given[i], max(1, budget * loads[i] // mass), spare)
            given[i] = given[i] + extra
            spare = spare - extra
    return np.array(given)


def normal_values(own_key, shape, deviation, limit, split=(), kind=jnp.bfloat16):
    entries = jax.random.normal(own_key, shape, jnp.float32) * deviation
    if len(split) > 0:
        entries = block_levels(own_key, shape, split, -0.22, 0.18) * entries
    return jnp.clip(entries, min=-limit, max=limit).astype(kind)


def setup_inputs(seed: int = 0, part: int = 0) -> dict:
    seeds = jax.random.split(jax.random.key(seed), 11)
    part_splits = jax.random.split(jax.random.fold_in(seeds[10], part), 11)
    tokens = normal_values(part_splits[0], (SEQ_LEN, D), 1.0, 6.0, ((0, 64),))
    norm_gain = jnp.clip(1.0 + 0.18 * jax.random.normal(seeds[1], (D,), jnp.float32), 0.1, 1.9)
    qkv_weight = draw_qkv_weight(jax.random.fold_in(seeds[10], 71), part)
    sinks = jnp.clip(jax.random.uniform(seeds[3], (QH,), jnp.float32, 0.0, 5.0), 0.0, 5.0)
    out_weight = normal_values(seeds[4], (QH * HD, D), (QH * HD) ** -0.5, 0.125, ((0, 64),))
    moe_gain = jnp.clip(1.0 + 0.18 * jax.random.normal(seeds[5], (D,), jnp.float32), 0.1, 1.9)
    expert_in = normal_values(seeds[6], (EXPERTS, D, 2 * H), D ** -0.5, 0.15625, ((0, 64),))
    expert_out = normal_values(seeds[7], (EXPERTS, H, D), H ** -0.5, 0.15625, ((0, 64),))
    expert_ids_keys = jax.random.split(jax.random.fold_in(part_splits[8], 1), SEQ_LEN // TOK_DEV)
    expert_ids_turns = jax.random.permutation(jax.random.fold_in(part_splits[8], 3), SEQ_LEN // TOK_DEV)
    expert_ids = jax.vmap(lambda own, number: routed_block(jax.random.fold_in(part_splits[8], 2), own, number, TOK_DEV, EXPERTS, TOP, CAP, 2))(expert_ids_keys, expert_ids_turns).reshape((SEQ_LEN, TOP))
    gate_ints = place_ends(jax.random.randint(part_splits[9], (SEQ_LEN, TOP), 1, 4097), jax.random.fold_in(part_splits[9], 1), 1, 4096).astype(jnp.int32)
    return dict(tokens=tokens, norm_gain=norm_gain, qkv_weight=qkv_weight, sinks=sinks, out_weight=out_weight, moe_gain=moe_gain, expert_in=expert_in, expert_out=expert_out, expert_ids=expert_ids, gate_ints=gate_ints)


epsilon = 1e-05
rope_base = 150000.0
glu_slope = 1.702

def norm_scale(values, gain):
    widened = values.astype(jnp.float32)
    mean_sq = lax.optimization_barrier(jnp.mean(widened * widened, axis=-1, keepdims=True))
    return widened * lax.rsqrt(mean_sq + epsilon) * gain.astype(jnp.float32)

def rotate(values, positions):
    half_width = values.shape[-1] // 2
    freq_steps = jnp.arange(half_width).astype(jnp.float32)
    inverse = jnp.exp(freq_steps * (-2.0 * math.log(rope_base) / values.shape[-1]))
    angles = positions[:, None] * inverse[None, :]
    cosine = jnp.cos(angles)[:, None, :]
    sine_term = jnp.sin(angles)[:, None, :]
    lower_half = values[..., :half_width]
    second = values[..., half_width:]
    return jnp.concatenate([lower_half * cosine - second * sine_term, second * cosine + lower_half * sine_term], axis=-1)

def band_block(queries, key_heads, value_heads, sinks, first_pos):
    count = queries.shape[0]
    groups = QH // KVH
    grouped = queries.reshape(count, KVH, groups, HD).astype(jnp.float32)
    scores = jnp.einsum('tkgd,skd->kgts', grouped, key_heads.astype(jnp.float32)) * (1.0 / math.sqrt(HD))
    query_pos = first_pos + jnp.arange(count).astype(jnp.int32)
    key_pos = first_pos - count + jnp.arange(2 * count).astype(jnp.int32)
    distance = query_pos[:, None] - key_pos[None, :]
    allowed = (distance >= 0) & (distance < WIN) & (key_pos >= 0)[None, :]
    scores = jnp.where(allowed[None, None, :, :], scores, -jnp.inf)
    sink_logit = sinks.reshape(KVH, groups, 1, 1).astype(jnp.float32)
    row_peak = jnp.maximum(lax.optimization_barrier(jnp.max(scores, axis=-1, keepdims=True)), sink_logit)
    raised = jnp.exp(scores - row_peak)
    totals = lax.optimization_barrier(jnp.sum(raised, axis=-1, keepdims=True)) + jnp.exp(sink_logit - row_peak)
    weights = (raised / totals).astype(jnp.bfloat16)
    mixture = jnp.einsum('kgts,skd->tkgd', weights.astype(jnp.float32), value_heads.astype(jnp.float32))
    return mixture.reshape(count, QH * HD).astype(jnp.bfloat16)

def reference(tokens, norm_gain, qkv_weight, sinks, out_weight, moe_gain, expert_in, expert_out, expert_ids, gate_ints):
    seq_len = tokens.shape[0]
    local_rows = TOK_DEV
    query_cols = QH * HD
    key_cols = KVH * HD
    residual = tokens.astype(jnp.float32)
    normed = norm_scale(tokens, norm_gain).astype(jnp.bfloat16)
    projections = jnp.dot(normed, qkv_weight, preferred_element_type=jnp.float32)
    positions = jnp.arange(seq_len).astype(jnp.float32)
    queries = rotate(projections[:, :query_cols].reshape(seq_len, QH, HD), positions).astype(jnp.bfloat16)
    key_heads = rotate(projections[:, query_cols:query_cols + key_cols].reshape(seq_len, KVH, HD), positions).astype(jnp.bfloat16)
    value_heads = projections[:, query_cols + key_cols:].reshape(seq_len, KVH, HD).astype(jnp.bfloat16)
    padding = jnp.zeros((local_rows, KVH, HD), jnp.bfloat16)
    prev_keys = jnp.concatenate([padding, key_heads[:seq_len - local_rows]], axis=0).reshape(N_SEQ, local_rows, KVH, HD)
    prev_values = jnp.concatenate([padding, value_heads[:seq_len - local_rows]], axis=0).reshape(N_SEQ, local_rows, KVH, HD)
    key_blocks = jnp.concatenate([prev_keys, key_heads.reshape(N_SEQ, local_rows, KVH, HD)], axis=1)
    value_blocks = jnp.concatenate([prev_values, value_heads.reshape(N_SEQ, local_rows, KVH, HD)], axis=1)
    query_blocks = queries.reshape(N_SEQ, local_rows, QH, HD)
    starts = (jnp.arange(N_SEQ) * local_rows).astype(jnp.int32)

    def attend(element):
        return band_block(element[0], element[1], element[2], sinks, element[3])
    attention = lax.map(attend, (query_blocks, key_blocks, value_blocks, starts)).reshape(seq_len, query_cols)
    projected = jnp.dot(attention, out_weight, preferred_element_type=jnp.float32)
    residual_mid = (residual + projected).astype(jnp.bfloat16)
    moe_input = norm_scale(residual_mid, moe_gain).astype(jnp.bfloat16)
    id_blocks = expert_ids.reshape(N_SEQ, local_rows * TOP)
    onehot = (id_blocks[:, :, None] == jnp.arange(EXPERTS).astype(jnp.int32)[None, None, :]).astype(jnp.int32)
    before = jnp.cumsum(onehot, axis=1) - onehot
    slot_index = lax.optimization_barrier(jnp.sum(before * onehot, axis=2))
    expert_rows = N_SEQ * CAP
    target = (id_blocks * expert_rows + jnp.arange(N_SEQ).astype(jnp.int32)[:, None] * CAP + slot_index).reshape(-1).astype(jnp.int32)
    source = jnp.repeat(moe_input, TOP, axis=0)
    buffer = jnp.zeros((EXPERTS * expert_rows, tokens.shape[1]), jnp.bfloat16).at[target].set(source)

    def expert(element):
        slab, weight_in, weight_out = element
        paired = jnp.dot(slab, weight_in, preferred_element_type=jnp.float32)
        gate_part = paired[:, :H]
        up_part = paired[:, H:]
        activated = (gate_part * jax.nn.sigmoid(glu_slope * gate_part) * (up_part + 1.0)).astype(jnp.bfloat16)
        return jnp.dot(activated, weight_out, preferred_element_type=jnp.float32).astype(jnp.bfloat16)
    results = lax.map(expert, (buffer.reshape(EXPERTS, expert_rows, tokens.shape[1]), expert_in, expert_out))
    picked = results.reshape(EXPERTS * expert_rows, tokens.shape[1])[target].reshape(seq_len, TOP, tokens.shape[1])
    route_weight = gate_ints.astype(jnp.float32)
    route_weight = route_weight / lax.optimization_barrier(jnp.sum(route_weight, axis=-1, keepdims=True))
    combined = lax.optimization_barrier(jnp.sum(picked.astype(jnp.float32) * route_weight[:, :, None], axis=1))
    return (residual_mid.astype(jnp.float32) + combined).astype(jnp.bfloat16)
```

```python
import math

import jax
import jax.numpy as jnp
from jax import lax
from jax.sharding import PartitionSpec as P

QH = 32
KVH = 4
HD = 64
WIN = 128
TOP = 4


epsilon = 1e-05
rope_base = 150000.0
glu_slope = 1.702


def shifted(value, axis, steps):
    count = lax.axis_size(axis)
    initial, last = (max(0, -steps), min(count, count - steps))
    return lax.ppermute(value, axis, [(source, source + steps) for source in range(initial, last)])


def norm_scale(values, gain):
    widened = values.astype(jnp.float32)
    mean_sq = jnp.mean(widened * widened, axis=-1, keepdims=True)
    return widened * lax.rsqrt(mean_sq + epsilon) * gain


def rotate(values, positions):
    half_width = values.shape[-1] // 2
    freq_steps = jnp.arange(half_width).astype(jnp.float32)
    inverse = jnp.exp(freq_steps * (-2.0 * math.log(rope_base) / values.shape[-1]))
    angles = positions[:, None] * inverse[None, :]
    cosine = jnp.cos(angles)[:, None, :]
    sine_term = jnp.sin(angles)[:, None, :]
    lower_half = values[..., :half_width]
    second = values[..., half_width:]
    return jnp.concatenate(
        [lower_half * cosine - second * sine_term, second * cosine + lower_half * sine_term],
        axis=-1,
    )


def band_block(queries, key_heads, value_heads, sinks, first_pos):
    count = queries.shape[0]
    groups = QH // KVH
    grouped = queries.reshape(count, KVH, groups, HD)
    scores = jnp.einsum(
        "tkgd,skd->kgts", grouped, key_heads, preferred_element_type=jnp.float32
    ) * (1.0 / math.sqrt(HD))
    query_pos = first_pos + jnp.arange(count)
    key_pos = first_pos - count + jnp.arange(2 * count)
    distance = query_pos[:, None] - key_pos[None, :]
    allowed = (distance >= 0) & (distance < WIN) & (key_pos >= 0)[None, :]
    scores = jnp.where(allowed[None, None, :, :], scores, -jnp.inf)
    sink_logit = sinks.reshape(KVH, groups, 1, 1)
    row_peak = jnp.maximum(jnp.max(scores, axis=-1, keepdims=True), sink_logit)
    raised = jnp.exp(scores - row_peak)
    totals = jnp.sum(raised, axis=-1, keepdims=True) + jnp.exp(sink_logit - row_peak)
    weights = (raised / totals).astype(jnp.bfloat16)
    mixture = jnp.einsum("kgts,skd->tkgd", weights, value_heads, preferred_element_type=jnp.float32)
    return mixture.reshape(count, QH * HD).astype(jnp.bfloat16)


def run_expert(incoming, weight_in, weight_out):
    width = incoming.shape[-1]
    hidden_width = weight_in.shape[1] // 2
    flat_rows = incoming.reshape(-1, width)
    paired = jnp.dot(flat_rows, weight_in, preferred_element_type=jnp.float32)
    gate_part = paired[:, :hidden_width]
    up_part = paired[:, hidden_width:]
    activated = (gate_part * jax.nn.sigmoid(glu_slope * gate_part) * (up_part + 1.0)).astype(
        jnp.bfloat16
    )
    produced = jnp.dot(activated, weight_out, preferred_element_type=jnp.float32).astype(
        jnp.bfloat16
    )
    return produced.reshape(incoming.shape)


def route_slots(expert_ids, devices, capacity):
    rows = expert_ids.shape[0]
    flat_ids = expert_ids.reshape(-1)
    onehot = (flat_ids[:, None] == jnp.arange(devices)[None, :]).astype(jnp.int32)
    before = jnp.cumsum(onehot, axis=0) - onehot
    slot_index = jnp.sum(before * onehot, axis=1)
    return (flat_ids * capacity + slot_index).reshape(rows, TOP)


def local(
    tokens,
    norm_gain,
    qkv_weight,
    sinks,
    out_weight,
    moe_gain,
    expert_in,
    expert_out,
    expert_ids,
    gate_ints,
):
    local_rows = tokens.shape[0]
    width = tokens.shape[1]
    devices = lax.axis_size("seq")
    device_index = lax.axis_index("seq")
    capacity = 2 * local_rows * TOP // devices
    query_cols = QH * HD
    key_cols = KVH * HD
    qkv_part = qkv_weight.shape[1]

    residual = tokens.astype(jnp.float32)
    normed = norm_scale(tokens, norm_gain).astype(jnp.bfloat16)
    both = jnp.concatenate([qkv_weight.T, out_weight], axis=0)
    gathered = lax.all_gather(both, "seq", axis=0)
    projections = lax.dot_general(
        normed,
        gathered[:, :qkv_part].reshape(-1, width),
        (((1,), (1,)), ((), ())),
        preferred_element_type=jnp.float32,
    )
    first_pos = device_index * local_rows
    positions = (first_pos + jnp.arange(local_rows)).astype(jnp.float32)
    queries = rotate(projections[:, :query_cols].reshape(local_rows, QH, HD), positions).astype(
        jnp.bfloat16
    )
    key_heads = rotate(
        projections[:, query_cols : query_cols + key_cols].reshape(local_rows, KVH, HD), positions
    ).astype(jnp.bfloat16)
    value_heads = (
        projections[:, query_cols + key_cols :].reshape(local_rows, KVH, HD).astype(jnp.bfloat16)
    )
    prev_keys, prev_values = shifted((key_heads, value_heads), "seq", 1)
    key_block = jnp.concatenate([prev_keys, key_heads], axis=0)
    value_block = jnp.concatenate([prev_values, value_heads], axis=0)
    attention = band_block(queries, key_block, value_block, sinks, first_pos)
    projected = jnp.dot(
        attention,
        gathered[:, qkv_part:].reshape(-1, width),
        preferred_element_type=jnp.float32,
    )
    residual_mid = (residual + projected).astype(jnp.bfloat16)
    moe_input = norm_scale(residual_mid, moe_gain).astype(jnp.bfloat16)

    target = route_slots(expert_ids, devices, capacity)
    route_weight = gate_ints.astype(jnp.float32)
    route_weight = route_weight / jnp.sum(route_weight, axis=-1, keepdims=True)
    halves = 2
    slots = devices * capacity // halves
    depth = capacity // halves

    def places_of(half):
        row = jnp.arange(slots)
        return row // depth * capacity + half * depth + row % depth

    combined = residual_mid.astype(jnp.float32)
    arrived = []
    for half in range(halves):
        places = places_of(half)
        pick = sum(
            (target[:, which][None, :] == places[:, None]).astype(jnp.bfloat16)
            for which in range(TOP)
        )
        rows = jnp.dot(pick, moe_input, preferred_element_type=jnp.float32).astype(jnp.bfloat16)
        rows = rows.reshape(devices, depth, width)
        arrived.append(lax.all_to_all(rows, "seq", split_axis=0, concat_axis=0, tiled=True))
    for half in range(halves):
        made = run_expert(arrived[half], expert_in[0], expert_out[0])
        back = lax.all_to_all(made, "seq", split_axis=0, concat_axis=0, tiled=True)
        places = places_of(half)
        share = sum(
            jnp.where(
                target[:, which][:, None] == places[None, :], route_weight[:, which : which + 1], 0.0
            )
            for which in range(TOP)
        )
        coarse = share.astype(jnp.bfloat16)
        fine = (share - coarse.astype(jnp.float32)).astype(jnp.bfloat16)
        flat = back.reshape(slots, width)
        combined = combined + (
            jnp.dot(coarse, flat, preferred_element_type=jnp.float32)
            + jnp.dot(fine, flat, preferred_element_type=jnp.float32)
        )
    return combined.astype(jnp.bfloat16)


def solution(mesh):
    return jax.shard_map(
        local,
        mesh=mesh,
        in_specs=(
            P(("batch", "seq"), None),
            P(),
            P(None, "seq"),
            P(),
            P("seq", None),
            P(),
            P("seq", None, None),
            P("seq", None, None),
            P(("batch", "seq"), None),
            P(("batch", "seq"), None),
        ),
        out_specs=P(("batch", "seq"), None),
        check_vma=False,
    )
```

```python
import math

import jax
import jax.numpy as jnp
from jax import lax
from jax.experimental import pallas as pl
from jax.experimental.pallas import tpu as pltpu
from jax.sharding import Mesh
from jax.sharding import PartitionSpec as P

QH = 32
KVH = 4
HD = 64
WIN = 128
TOP = 4


epsilon = 1e-05
rope_base = 150000.0
glu_slope = 1.702
SEQ = ("z", "y", "c")
PLANE = ("y", "c")
CAP = 16
META = 16
VMEM_LIMIT = 48 * 1024 * 1024


def shifted(value, axis, steps):
    count = math.prod(lax.axis_size(name) for name in axis)
    initial, last = (max(0, -steps), min(count, count - steps))
    return lax.ppermute(value, axis, [(source, source + steps) for source in range(initial, last)])


def norm_scale(values, gain):
    widened = values.astype(jnp.float32)
    mean_sq = jnp.mean(widened * widened, axis=-1, keepdims=True)
    return widened * lax.rsqrt(mean_sq + epsilon) * gain


def rotate(values, positions):
    half_width = values.shape[-1] // 2
    freq_steps = jnp.arange(half_width).astype(jnp.float32)
    inverse = jnp.exp(freq_steps * (-2.0 * math.log(rope_base) / values.shape[-1]))
    angles = positions[:, None] * inverse[None, :]
    cosine = jnp.cos(angles)[:, None, :]
    sine_term = jnp.sin(angles)[:, None, :]
    lower_half = values[..., :half_width]
    second = values[..., half_width:]
    return jnp.concatenate(
        [lower_half * cosine - second * sine_term, second * cosine + lower_half * sine_term],
        axis=-1,
    )


def band_block(queries, key_heads, value_heads, sinks, first_pos):
    count = queries.shape[0]
    groups = QH // KVH
    grouped = queries.reshape(count, KVH, groups, HD)
    scores = jnp.einsum(
        "tkgd,skd->kgts", grouped, key_heads, preferred_element_type=jnp.float32
    ) * (1.0 / math.sqrt(HD))
    query_pos = first_pos + jnp.arange(count)
    key_pos = first_pos - count + jnp.arange(2 * count)
    distance = query_pos[:, None] - key_pos[None, :]
    allowed = (distance >= 0) & (distance < WIN) & (key_pos >= 0)[None, :]
    scores = jnp.where(allowed[None, None, :, :], scores, -jnp.inf)
    sink_logit = sinks.reshape(KVH, groups, 1, 1)
    row_peak = jnp.maximum(jnp.max(scores, axis=-1, keepdims=True), sink_logit)
    raised = jnp.exp(scores - row_peak)
    totals = jnp.sum(raised, axis=-1, keepdims=True) + jnp.exp(sink_logit - row_peak)
    weights = (raised / totals).astype(jnp.bfloat16)
    mixture = jnp.einsum("kgts,skd->tkgd", weights, value_heads, preferred_element_type=jnp.float32)
    return mixture.reshape(count, QH * HD).astype(jnp.bfloat16)


def whole(count):
    return [pl.BlockSpec(memory_space=pltpu.VMEM)] * count


def local_call(body, out_shape, in_specs, scratch_shapes=()):
    outs = jax.tree.leaves(out_shape)
    return pl.pallas_call(
        body,
        out_shape=out_shape,
        in_specs=in_specs,
        out_specs=jax.tree.map(lambda _: pl.BlockSpec(memory_space=pltpu.VMEM), out_shape)
        if len(outs) > 1
        else pl.BlockSpec(memory_space=pltpu.VMEM),
        scratch_shapes=scratch_shapes,
        compiler_params=pltpu.CompilerParams(vmem_limit_bytes=VMEM_LIMIT),
    )


def slot_match(meta, first_expert, which):
    ids = meta[:, which : which + 1] - first_expert
    places = ids * float(CAP) + meta[:, TOP + which : TOP + which + 1]
    columns = lax.broadcasted_iota(jnp.int32, (meta.shape[0], 8 * CAP), 1).astype(jnp.float32)
    return columns == places


def select_rows(block, width, first_expert):
    meta = block[:, width : width + META].astype(jnp.float32)
    pick = jnp.zeros((block.shape[0], 8 * CAP), jnp.float32)
    for which in range(TOP):
        pick = jnp.where(slot_match(meta, first_expert, which), 1.0, pick)
    return lax.dot_general(
        pick.astype(jnp.bfloat16),
        block[:, :width],
        (((0,), (0,)), ((), ())),
        preferred_element_type=jnp.float32,
    ).astype(jnp.bfloat16)


def weigh_rows(block, width, first_expert, rows):
    meta = block[:, width : width + META].astype(jnp.float32)
    coarse = jnp.zeros((block.shape[0], 8 * CAP), jnp.float32)
    fine = coarse
    for which in range(TOP):
        here = slot_match(meta, first_expert, which)
        coarse = jnp.where(here, meta[:, 2 * TOP + which : 2 * TOP + which + 1], coarse)
        fine = jnp.where(here, meta[:, 3 * TOP + which : 3 * TOP + which + 1], fine)
    return jnp.dot(
        coarse.astype(jnp.bfloat16), rows, preferred_element_type=jnp.float32
    ) + jnp.dot(fine.astype(jnp.bfloat16), rows, preferred_element_type=jnp.float32)


def dispatch_rows(plane, blocks, width):
    count = len(blocks)

    def body(plane_ref, *refs):
        out_ref = refs[-1]
        first_expert = (plane_ref[0] * 8).astype(jnp.float32)
        for number in range(count):
            rows = select_rows(refs[number][...], width, first_expert)
            out_ref[:, number * CAP : (number + 1) * CAP, :] = rows.reshape(8, CAP, width)

    return local_call(
        body,
        jax.ShapeDtypeStruct((8, count * CAP, width), jnp.bfloat16),
        [pl.BlockSpec(memory_space=pltpu.SMEM)] + whole(count),
    )(plane, *blocks)


def run_expert(groups, weight_in, weight_out):
    width = groups[0].shape[-1]
    hidden = weight_out.shape[1]
    flat = [group.reshape(-1, width) for group in groups]
    sizes = [rows.shape[0] for rows in flat]
    total = sum(sizes)
    ends = list(range(0, width, 384)) + [width]
    spans = list(zip(ends, ends[1:]))

    def body(*refs):
        ins, (in_hbm, out_hbm) = refs[: len(flat)], refs[len(flat) : len(flat) + 2]
        outs = refs[len(flat) + 2 : 2 * len(flat) + 2]
        in_ref, out_ref, rows_ref, acc_ref, sems = refs[2 * len(flat) + 2 :]
        copies = [
            pltpu.make_async_copy(
                in_hbm.at[0, pl.ds(low, high - low)], in_ref.at[pl.ds(low, high - low)], sems.at[n]
            )
            for n, (low, high) in enumerate(spans)
        ]
        copies.append(pltpu.make_async_copy(out_hbm.at[0], out_ref, sems.at[len(spans)]))
        for copy in copies:
            copy.start()
        start = 0
        for size, rows in zip(sizes, ins):
            rows_ref[start : start + size] = rows[...]
            start += size
        for n, (low, high) in enumerate(spans):
            copies[n].wait()
            part = jnp.dot(
                rows_ref[:, low:high], in_ref[low:high], preferred_element_type=jnp.float32
            )
            if n == 0:
                acc_ref[...] = part
            else:
                acc_ref[...] += part
        gate_part = acc_ref[:, :hidden]
        up_part = acc_ref[:, hidden:]
        activated = (
            gate_part * (1.0 / (1.0 + jnp.exp(-glu_slope * gate_part))) * (up_part + 1.0)
        ).astype(jnp.bfloat16)
        copies[-1].wait()
        made = jnp.dot(activated, out_ref[...], preferred_element_type=jnp.float32).astype(
            jnp.bfloat16
        )
        start = 0
        for size, place in zip(sizes, outs):
            place[...] = made[start : start + size]
            start += size

    made = pl.pallas_call(
        body,
        out_shape=[jax.ShapeDtypeStruct(rows.shape, jnp.bfloat16) for rows in flat],
        in_specs=whole(len(flat)) + [pl.BlockSpec(memory_space=pltpu.HBM)] * 2,
        out_specs=whole(len(flat)),
        scratch_shapes=[
            pltpu.VMEM((width, 2 * hidden), jnp.bfloat16),
            pltpu.VMEM((hidden, width), jnp.bfloat16),
            pltpu.VMEM((total, width), jnp.bfloat16),
            pltpu.VMEM((total, 2 * hidden), jnp.float32),
            pltpu.SemaphoreType.DMA((len(spans) + 1,)),
        ],
        compiler_params=pltpu.CompilerParams(vmem_limit_bytes=VMEM_LIMIT),
    )(*flat, weight_in, weight_out)
    return [rows.reshape(group.shape) for rows, group in zip(made, groups)]


def combine_far(plane, block, rows, width):
    half = block.shape[0] // 2

    def body(plane_ref, block_ref, rows_ref, low_ref, high_ref):
        first_expert = (plane_ref[0] * 8).astype(jnp.float32)
        summed = weigh_rows(
            block_ref[...], width, first_expert, rows_ref[...].reshape(8 * CAP, width)
        ).astype(jnp.bfloat16)
        low_ref[...] = summed[:half]
        high_ref[...] = summed[half:]

    return local_call(
        body,
        [jax.ShapeDtypeStruct((half, width), jnp.bfloat16)] * 2,
        [pl.BlockSpec(memory_space=pltpu.SMEM)] + whole(2),
    )(plane, block, rows)


def combine_pair(plane, blocks, rows, arrived, width):
    count = blocks[0].shape[0]

    def body(plane_ref, low_ref, high_ref, rows_ref, first_ref, second_ref, *outs):
        first_expert = (plane_ref[0] * 8).astype(jnp.float32)
        for number, (block, came) in enumerate(((low_ref, first_ref), (high_ref, second_ref))):
            part = rows_ref[:, number * CAP : (number + 1) * CAP, :].reshape(8 * CAP, width)
            summed = weigh_rows(block[...], width, first_expert, part)
            size = came.shape[0]
            if size == count:
                outs[number][...] = (summed + came[...].astype(jnp.float32)).astype(jnp.bfloat16)
            else:
                at = number * size
                other = size - at
                outs[number][at : at + size] = (
                    summed[at : at + size] + came[...].astype(jnp.float32)
                ).astype(jnp.bfloat16)
                outs[number][other : other + size] = summed[other : other + size].astype(
                    jnp.bfloat16
                )

    return local_call(
        body,
        [jax.ShapeDtypeStruct((count, width), jnp.bfloat16)] * 2,
        [pl.BlockSpec(memory_space=pltpu.SMEM)] + whole(5),
    )(plane, *blocks, rows, *arrived)


def combine_last(plane, block, rows, arrived, residual_mid, width):
    def body(plane_ref, block_ref, rows_ref, first_ref, second_ref, residual_ref, out_ref):
        first_expert = (plane_ref[0] * 8).astype(jnp.float32)
        summed = weigh_rows(
            block_ref[...], width, first_expert, rows_ref[...].reshape(8 * CAP, width)
        )
        out_ref[...] = (
            residual_ref[...].astype(jnp.float32)
            + summed
            + first_ref[...].astype(jnp.float32)
            + second_ref[...].astype(jnp.float32)
        ).astype(jnp.bfloat16)

    return local_call(
        body,
        jax.ShapeDtypeStruct(residual_mid.shape, jnp.bfloat16),
        [pl.BlockSpec(memory_space=pltpu.SMEM)] + whole(5),
    )(plane, block, rows, *arrived, residual_mid)


def routing_columns(expert_ids, gate_ints, experts):
    rows = expert_ids.shape[0]
    flat_ids = expert_ids.reshape(-1)
    onehot = (flat_ids[:, None] == jnp.arange(experts)[None, :]).astype(jnp.int32)
    before = jnp.cumsum(onehot, axis=0) - onehot
    slot_index = jnp.sum(before * onehot, axis=1).reshape(rows, TOP)
    route_weight = gate_ints.astype(jnp.float32)
    route_weight = route_weight / jnp.sum(route_weight, axis=-1, keepdims=True)
    coarse = lax.reduce_precision(route_weight, 8, 7)
    fine = route_weight - coarse
    return jnp.concatenate(
        [expert_ids.astype(jnp.float32), slot_index.astype(jnp.float32), coarse, fine], axis=1
    ).astype(jnp.bfloat16)


def local(
    tokens,
    norm_gain,
    qkv_weight,
    sinks,
    out_weight,
    moe_gain,
    expert_in,
    expert_out,
    expert_ids,
    gate_ints,
):
    local_rows = tokens.shape[0]
    width = tokens.shape[1]
    devices = math.prod(lax.axis_size(name) for name in SEQ)
    device_index = lax.axis_index(SEQ)
    query_cols = QH * HD
    key_cols = KVH * HD
    qkv_part = qkv_weight.shape[1]

    residual = tokens.astype(jnp.float32)
    normed = norm_scale(tokens, norm_gain).astype(jnp.bfloat16)
    both = jnp.concatenate([qkv_weight.T, out_weight], axis=0)
    gathered = lax.all_gather(both, SEQ, axis=0)
    projections = lax.dot_general(
        normed,
        gathered[:, :qkv_part].reshape(-1, width),
        (((1,), (1,)), ((), ())),
        preferred_element_type=jnp.float32,
    )
    first_pos = device_index * local_rows
    positions = (first_pos + jnp.arange(local_rows)).astype(jnp.float32)
    queries = rotate(projections[:, :query_cols].reshape(local_rows, QH, HD), positions).astype(
        jnp.bfloat16
    )
    key_heads = rotate(
        projections[:, query_cols : query_cols + key_cols].reshape(local_rows, KVH, HD), positions
    ).astype(jnp.bfloat16)
    value_heads = (
        projections[:, query_cols + key_cols :].reshape(local_rows, KVH, HD).astype(jnp.bfloat16)
    )
    prev_keys, prev_values = shifted((key_heads, value_heads), SEQ, 1)
    key_block = jnp.concatenate([prev_keys, key_heads], axis=0)
    value_block = jnp.concatenate([prev_values, value_heads], axis=0)
    attention = band_block(queries, key_block, value_block, sinks, first_pos)
    projected = jnp.dot(
        attention,
        gathered[:, qkv_part:].reshape(-1, width),
        preferred_element_type=jnp.float32,
    )
    residual_mid = (residual + projected).astype(jnp.bfloat16)
    moe_input = norm_scale(residual_mid, moe_gain).astype(jnp.bfloat16)

    columns = routing_columns(expert_ids, gate_ints, devices)
    own = jnp.concatenate([moe_input, columns], axis=1)

    planes = lax.axis_size("z")
    half = local_rows // 2
    plane = lax.axis_index("z").astype(jnp.int32).reshape(1)
    forward = [(at, (at + 1) % planes) for at in range(planes)]
    backward = [(at, (at - 1) % planes) for at in range(planes)]

    def plane_exchange(rows):
        return lax.all_to_all(rows, PLANE, split_axis=0, concat_axis=0, tiled=True)

    weight_in = pltpu.with_memory_space_constraint(expert_in, pltpu.HBM)
    weight_out = pltpu.with_memory_space_constraint(expert_out, pltpu.HBM)

    def pass_on(rows, perm):
        return lax.ppermute(rows, "z", perm)

    rising, falling = [own], [own]
    for _ in range(3):
        rising.append(pass_on(rising[-1], forward))
        falling.append(pass_on(falling[-1], backward))
    far = jnp.concatenate(
        [pass_on(rising[3][:half], forward), pass_on(falling[3][half:], backward)],
        axis=0,
    )
    near = [own, rising[1], falling[1]]
    groups = (near, [rising[2], falling[2]], [rising[3], falling[3]], [far])
    made = []
    for group in groups:
        rows = dispatch_rows(plane, group, width)
        rows = plane_exchange(rows)
        made += run_expert([rows], weight_in, weight_out)
    back = [plane_exchange(made[number]) for number in range(4)]

    to_rising, to_falling = combine_far(plane, far, back[3], width)
    for step in (3, 2, 1):
        to_rising = pass_on(to_rising, backward)
        to_falling = pass_on(to_falling, forward)
        rows = back[step - 1]
        to_rising, to_falling = combine_pair(
            plane,
            (rising[step], falling[step]),
            rows[:, CAP:] if step == 1 else rows,
            (to_rising, to_falling),
            width,
        )
    to_rising = pass_on(to_rising, backward)
    to_falling = pass_on(to_falling, forward)
    return combine_last(
        plane, own, back[0][:, :CAP], (to_rising, to_falling), residual_mid, width
    )


def solution(mesh):
    grid = Mesh(mesh.devices.reshape(8, 4, 2, 4), ("z", "y", "c", "x"))
    rows = P(("x", *SEQ), None)
    return jax.shard_map(
        local,
        mesh=grid,
        in_specs=(
            rows,
            P(),
            P(None, SEQ),
            P(),
            P(SEQ, None),
            P(),
            P(SEQ, None, None),
            P(SEQ, None, None),
            rows,
            rows,
        ),
        out_specs=rows,
        check_vma=False,
    )
```

```python
import math

import jax
import jax.numpy as jnp
from jax import lax
from jax.experimental import pallas as pl
from jax.experimental.pallas import tpu as pltpu
from jax.sharding import Mesh
from jax.sharding import PartitionSpec as P

QH = 32
KVH = 4
HD = 64
WIN = 128
TOP = 4


epsilon = 1e-05
rope_base = 150000.0
glu_slope = 1.702
SEQ = ("z", "y", "c")
PLANE = ("y", "c")
CAP = 16
META = 3 * TOP
TILE = 128
SPAN = 384
VMEM_LIMIT = 48 * 1024 * 1024


def shifted(value, axis, steps):
    count = math.prod(lax.axis_size(name) for name in axis)
    initial, last = (max(0, -steps), min(count, count - steps))
    return lax.ppermute(value, axis, [(source, source + steps) for source in range(initial, last)])


def norm_scale(values, gain):
    widened = values.astype(jnp.float32)
    mean_sq = jnp.mean(widened * widened, axis=-1, keepdims=True)
    return widened * lax.rsqrt(mean_sq + epsilon) * gain


def rotate(values, positions):
    half_width = values.shape[-1] // 2
    freq_steps = jnp.arange(half_width).astype(jnp.float32)
    inverse = jnp.exp(freq_steps * (-2.0 * math.log(rope_base) / values.shape[-1]))
    angles = positions[:, None] * inverse[None, :]
    cosine = jnp.cos(angles)[:, None, :]
    sine_term = jnp.sin(angles)[:, None, :]
    lower_half = values[..., :half_width]
    second = values[..., half_width:]
    return jnp.concatenate(
        [lower_half * cosine - second * sine_term, second * cosine + lower_half * sine_term],
        axis=-1,
    )


def band_block(queries, key_heads, value_heads, sinks, first_pos):
    count = queries.shape[0]
    groups = QH // KVH
    grouped = queries.reshape(count, KVH, groups, HD)
    scores = jnp.einsum(
        "tkgd,skd->kgts", grouped, key_heads, preferred_element_type=jnp.float32
    ) * (1.0 / math.sqrt(HD))
    query_pos = first_pos + jnp.arange(count)
    key_pos = first_pos - count + jnp.arange(2 * count)
    distance = query_pos[:, None] - key_pos[None, :]
    allowed = (distance >= 0) & (distance < WIN) & (key_pos >= 0)[None, :]
    scores = jnp.where(allowed[None, None, :, :], scores, -jnp.inf)
    sink_logit = sinks.reshape(KVH, groups, 1, 1)
    row_peak = jnp.maximum(jnp.max(scores, axis=-1, keepdims=True), sink_logit)
    raised = jnp.exp(scores - row_peak)
    totals = jnp.sum(raised, axis=-1, keepdims=True) + jnp.exp(sink_logit - row_peak)
    weights = (raised / totals).astype(jnp.bfloat16)
    mixture = jnp.einsum("kgts,skd->tkgd", weights, value_heads, preferred_element_type=jnp.float32)
    return mixture.reshape(count, QH * HD).astype(jnp.bfloat16)


def whole(count):
    return [pl.BlockSpec(memory_space=pltpu.VMEM)] * count


def local_call(body, out_shape, in_specs, scratch_shapes=()):
    outs = jax.tree.leaves(out_shape)
    return pl.pallas_call(
        body,
        out_shape=out_shape,
        in_specs=in_specs,
        out_specs=jax.tree.map(lambda _: pl.BlockSpec(memory_space=pltpu.VMEM), out_shape)
        if len(outs) > 1
        else pl.BlockSpec(memory_space=pltpu.VMEM),
        scratch_shapes=scratch_shapes,
        compiler_params=pltpu.CompilerParams(vmem_limit_bytes=VMEM_LIMIT),
    )


def slot_match(meta, first_expert, which):
    ids = meta[:, which : which + 1] - first_expert
    places = ids * float(CAP) + meta[:, TOP + which : TOP + which + 1]
    columns = lax.broadcasted_iota(jnp.int32, (meta.shape[0], 8 * CAP), 1).astype(jnp.float32)
    return columns == places


def select_rows(block, width, first_expert):
    meta = block[:, width : width + META].astype(jnp.float32)
    pick = jnp.zeros((block.shape[0], 8 * CAP), jnp.float32)
    for which in range(TOP):
        pick = jnp.where(slot_match(meta, first_expert, which), 1.0, pick)
    return lax.dot_general(
        pick.astype(jnp.bfloat16),
        block[:, :width],
        (((0,), (0,)), ((), ())),
        preferred_element_type=jnp.float32,
    ).astype(jnp.bfloat16)


def weigh_rows(block, width, first_expert, rows):
    meta = block[:, width : width + META].astype(jnp.float32)
    share = jnp.zeros((block.shape[0], 8 * CAP), jnp.float32)
    for which in range(TOP):
        share = jnp.where(
            slot_match(meta, first_expert, which),
            meta[:, 2 * TOP + which : 2 * TOP + which + 1],
            share,
        )
    return jnp.dot(share.astype(jnp.bfloat16), rows, preferred_element_type=jnp.float32)


def dispatch_rows(plane, blocks, width):
    count = len(blocks)

    def body(plane_ref, *refs):
        out_ref = refs[-1]
        first_expert = (plane_ref[0] * 8).astype(jnp.float32)
        for number in range(count):
            rows = select_rows(refs[number][...], width, first_expert)
            out_ref[:, number * CAP : (number + 1) * CAP, :] = rows.reshape(8, CAP, width)

    return local_call(
        body,
        jax.ShapeDtypeStruct((8, count * CAP, width), jnp.bfloat16),
        [pl.BlockSpec(memory_space=pltpu.SMEM)] + whole(count),
    )(plane, *blocks)


def run_expert(groups, parts, weight_in, weight_out):
    width = groups[0].shape[-1]
    hidden = weight_out.shape[1]
    total = sum(8 * group.shape[1] for group in groups)
    tiles = total // TILE
    count_in = width // SPAN
    rest = count_in * SPAN
    shapes = [(8, size, width) for sizes in parts for size in sizes]

    def body(*refs):
        ins, (in_hbm, out_hbm) = refs[: len(groups)], refs[len(groups) : len(groups) + 2]
        outs = refs[len(groups) + 2 : len(groups) + 2 + len(shapes)]
        in_ref, out_ref, rows_ref, acc_ref, sems = refs[len(groups) + 2 + len(shapes) :]

        def fetch(low, size, sem):
            return pltpu.make_async_copy(
                in_hbm.at[0, pl.ds(low, size)], in_ref.at[pl.ds(low, size)], sems.at[sem]
            )

        last = fetch(rest, width - rest, count_in)
        last.start()
        for n in range(count_in):
            fetch(n * SPAN, SPAN, n).start()
        down = pltpu.make_async_copy(out_hbm.at[0], out_ref, sems.at[count_in + 1])
        down.start()
        start = 0
        for rows in ins:
            count = 8 * rows.shape[1]
            rows_ref[start : start + count] = rows[...].reshape(count, width)
            start += count
        last.wait()

        def first(tile, carry):
            at = pl.ds(pl.multiple_of(tile * TILE, TILE), TILE)
            acc_ref[at] = jnp.dot(
                rows_ref[at, rest:], in_ref[rest:], preferred_element_type=jnp.float32
            )
            return carry

        lax.fori_loop(0, tiles, first, 0)

        def more(n, carry):
            low = pl.multiple_of(n * SPAN, SPAN)
            fetch(low, SPAN, n).wait()

            def multiply(tile, carry):
                at = pl.ds(pl.multiple_of(tile * TILE, TILE), TILE)
                acc_ref[at] += jnp.dot(
                    rows_ref[at, pl.ds(low, SPAN)],
                    in_ref[pl.ds(low, SPAN)],
                    preferred_element_type=jnp.float32,
                )
                return carry

            return lax.fori_loop(0, tiles, multiply, carry)

        lax.fori_loop(0, count_in, more, 0)
        down.wait()

        def finish(tile, carry):
            at = pl.ds(pl.multiple_of(tile * TILE, TILE), TILE)
            gate_part = acc_ref[at, :hidden]
            up_part = acc_ref[at, hidden:]
            activated = (
                gate_part * (1.0 / (1.0 + jnp.exp(-glu_slope * gate_part))) * (up_part + 1.0)
            ).astype(jnp.bfloat16)
            rows_ref[at] = jnp.dot(
                activated, out_ref[...], preferred_element_type=jnp.float32
            ).astype(jnp.bfloat16)
            return carry

        lax.fori_loop(0, tiles, finish, 0)
        start, place = 0, 0
        for group, sizes in zip(ins, parts):
            count = 8 * group.shape[1]
            made = rows_ref[start : start + count].reshape(8, group.shape[1], width)
            at = 0
            for size in sizes:
                outs[place][...] = made[:, at : at + size]
                at += size
                place += 1
            start += count

    return pl.pallas_call(
        body,
        out_shape=[jax.ShapeDtypeStruct(shape, jnp.bfloat16) for shape in shapes],
        in_specs=whole(len(groups)) + [pl.BlockSpec(memory_space=pltpu.HBM)] * 2,
        out_specs=whole(len(shapes)),
        scratch_shapes=[
            pltpu.VMEM((width, 2 * hidden), jnp.bfloat16),
            pltpu.VMEM((hidden, width), jnp.bfloat16),
            pltpu.VMEM((total, width), jnp.bfloat16),
            pltpu.VMEM((total, 2 * hidden), jnp.float32),
            pltpu.SemaphoreType.DMA((count_in + 2,)),
        ],
        compiler_params=pltpu.CompilerParams(vmem_limit_bytes=VMEM_LIMIT),
    )(*groups, weight_in, weight_out)


def project_in(tokens, gain, gathered, depth):
    count, width = tokens.shape
    shards = gathered.shape[0]
    chunks = 4
    step = shards // chunks

    def body(tokens_ref, gain_ref, gathered_hbm, out_ref, weight_ref, sems):
        copies = [
            pltpu.make_async_copy(
                gathered_hbm.at[pl.ds(n * step, step), pl.ds(0, depth)],
                weight_ref.at[pl.ds(n * step, step)],
                sems.at[n],
            )
            for n in range(chunks)
        ]
        for copy in copies:
            copy.start()
        normed = norm_scale(tokens_ref[...], gain_ref[...]).astype(jnp.bfloat16)
        for n, copy in enumerate(copies):
            copy.wait()
            weight = weight_ref[n * step : (n + 1) * step].reshape(step * depth, width)
            out_ref[:, n * step * depth : (n + 1) * step * depth] = lax.dot_general(
                normed, weight, (((1,), (1,)), ((), ())), preferred_element_type=jnp.float32
            )

    return pl.pallas_call(
        body,
        out_shape=jax.ShapeDtypeStruct((count, shards * depth), jnp.float32),
        in_specs=whole(2) + [pl.BlockSpec(memory_space=pltpu.HBM)],
        out_specs=pl.BlockSpec(memory_space=pltpu.VMEM),
        scratch_shapes=[
            pltpu.VMEM((shards, depth, width), jnp.bfloat16),
            pltpu.SemaphoreType.DMA((chunks,)),
        ],
        compiler_params=pltpu.CompilerParams(vmem_limit_bytes=VMEM_LIMIT),
    )(tokens, gain.reshape(1, width), gathered)


def project_out(attention, gathered, skip, tokens, gain, columns):
    count, width = tokens.shape
    shards, depth = gathered.shape[0], gathered.shape[1] - skip
    chunks = 4
    step = shards // chunks

    def body(attention_ref, gathered_hbm, tokens_ref, gain_ref, columns_ref, *refs):
        residual_ref, own_ref, weight_ref, sems = refs
        copies = [
            pltpu.make_async_copy(
                gathered_hbm.at[pl.ds(n * step, step), pl.ds(skip, depth)],
                weight_ref.at[pl.ds(n * step, step)],
                sems.at[n],
            )
            for n in range(chunks)
        ]
        for copy in copies:
            copy.start()
        total = tokens_ref[...].astype(jnp.float32)
        for n, copy in enumerate(copies):
            copy.wait()
            total += jnp.dot(
                attention_ref[:, n * step * depth : (n + 1) * step * depth],
                weight_ref[n * step : (n + 1) * step].reshape(step * depth, width),
                preferred_element_type=jnp.float32,
            )
        middle = total.astype(jnp.bfloat16)
        residual_ref[...] = middle
        own_ref[:, :width] = norm_scale(middle, gain_ref[...]).astype(jnp.bfloat16)
        own_ref[:, width:] = columns_ref[...]

    return pl.pallas_call(
        body,
        out_shape=[
            jax.ShapeDtypeStruct((count, width), jnp.bfloat16),
            jax.ShapeDtypeStruct((count, width + columns.shape[1]), jnp.bfloat16),
        ],
        in_specs=whole(1) + [pl.BlockSpec(memory_space=pltpu.HBM)] + whole(3),
        out_specs=whole(2),
        scratch_shapes=[
            pltpu.VMEM((shards, depth, width), jnp.bfloat16),
            pltpu.SemaphoreType.DMA((chunks,)),
        ],
        compiler_params=pltpu.CompilerParams(vmem_limit_bytes=VMEM_LIMIT),
    )(attention, gathered, tokens, gain.reshape(1, width), columns)


def combine_far(plane, block, rows, width):
    half = block.shape[0] // 2

    def body(plane_ref, block_ref, rows_ref, low_ref, high_ref):
        first_expert = (plane_ref[0] * 8).astype(jnp.float32)
        summed = weigh_rows(
            block_ref[...], width, first_expert, rows_ref[:, -CAP:, :].reshape(8 * CAP, width)
        ).astype(jnp.bfloat16)
        low_ref[...] = summed[:half]
        high_ref[...] = summed[half:]

    return local_call(
        body,
        [jax.ShapeDtypeStruct((half, width), jnp.bfloat16)] * 2,
        [pl.BlockSpec(memory_space=pltpu.SMEM)] + whole(2),
    )(plane, block, rows)


def combine_pair(plane, blocks, rows, arrived, width):
    count = blocks[0].shape[0]

    def body(plane_ref, low_ref, high_ref, rows_ref, first_ref, second_ref, *outs):
        first_expert = (plane_ref[0] * 8).astype(jnp.float32)
        for number, (block, came) in enumerate(((low_ref, first_ref), (high_ref, second_ref))):
            part = rows_ref[:, number * CAP : (number + 1) * CAP, :].reshape(8 * CAP, width)
            summed = weigh_rows(block[...], width, first_expert, part)
            size = came.shape[0]
            if size == count:
                outs[number][...] = (summed + came[...].astype(jnp.float32)).astype(jnp.bfloat16)
            else:
                at = number * size
                other = size - at
                outs[number][at : at + size] = (
                    summed[at : at + size] + came[...].astype(jnp.float32)
                ).astype(jnp.bfloat16)
                outs[number][other : other + size] = summed[other : other + size].astype(
                    jnp.bfloat16
                )

    return local_call(
        body,
        [jax.ShapeDtypeStruct((count, width), jnp.bfloat16)] * 2,
        [pl.BlockSpec(memory_space=pltpu.SMEM)] + whole(5),
    )(plane, *blocks, rows, *arrived)


def combine_last(plane, block, rows, arrived, residual_mid, width):
    def body(plane_ref, block_ref, rows_ref, first_ref, second_ref, residual_ref, out_ref):
        first_expert = (plane_ref[0] * 8).astype(jnp.float32)
        summed = weigh_rows(
            block_ref[...], width, first_expert, rows_ref[...].reshape(8 * CAP, width)
        )
        out_ref[...] = (
            residual_ref[...].astype(jnp.float32)
            + summed
            + first_ref[...].astype(jnp.float32)
            + second_ref[...].astype(jnp.float32)
        ).astype(jnp.bfloat16)

    return local_call(
        body,
        jax.ShapeDtypeStruct(residual_mid.shape, jnp.bfloat16),
        [pl.BlockSpec(memory_space=pltpu.SMEM)] + whole(5),
    )(plane, block, rows, *arrived, residual_mid)


def routing_columns(expert_ids, gate_ints, experts):
    rows = expert_ids.shape[0]
    flat_ids = expert_ids.reshape(-1)
    onehot = (flat_ids[:, None] == jnp.arange(experts)[None, :]).astype(jnp.int32)
    before = jnp.cumsum(onehot, axis=0) - onehot
    slot_index = jnp.sum(before * onehot, axis=1).reshape(rows, TOP)
    route_weight = gate_ints.astype(jnp.float32)
    route_weight = route_weight / jnp.sum(route_weight, axis=-1, keepdims=True)
    return jnp.concatenate(
        [expert_ids.astype(jnp.float32), slot_index.astype(jnp.float32), route_weight], axis=1
    ).astype(jnp.bfloat16)


def local(
    tokens,
    norm_gain,
    qkv_weight,
    sinks,
    out_weight,
    moe_gain,
    expert_in,
    expert_out,
    expert_ids,
    gate_ints,
):
    local_rows = tokens.shape[0]
    width = tokens.shape[1]
    devices = math.prod(lax.axis_size(name) for name in SEQ)
    device_index = lax.axis_index(SEQ)
    query_cols = QH * HD
    key_cols = KVH * HD
    qkv_part = qkv_weight.shape[1]

    both = jnp.concatenate([qkv_weight.T, out_weight], axis=0)
    gathered = lax.all_gather(both, SEQ, axis=0)
    projections = project_in(tokens, norm_gain, gathered, qkv_part)
    first_pos = device_index * local_rows
    positions = (first_pos + jnp.arange(local_rows)).astype(jnp.float32)
    queries = rotate(projections[:, :query_cols].reshape(local_rows, QH, HD), positions).astype(
        jnp.bfloat16
    )
    key_heads = rotate(
        projections[:, query_cols : query_cols + key_cols].reshape(local_rows, KVH, HD), positions
    ).astype(jnp.bfloat16)
    value_heads = (
        projections[:, query_cols + key_cols :].reshape(local_rows, KVH, HD).astype(jnp.bfloat16)
    )
    prev_keys, prev_values = shifted((key_heads, value_heads), SEQ, 1)
    key_block = jnp.concatenate([prev_keys, key_heads], axis=0)
    value_block = jnp.concatenate([prev_values, value_heads], axis=0)
    attention = band_block(queries, key_block, value_block, sinks, first_pos)
    columns = routing_columns(expert_ids, gate_ints, devices)
    residual_mid, own = project_out(
        attention,
        gathered,
        qkv_part,
        tokens,
        moe_gain,
        columns,
    )

    planes = lax.axis_size("z")
    half = local_rows // 2
    plane = lax.axis_index("z").astype(jnp.int32).reshape(1)
    forward = [(at, (at + 1) % planes) for at in range(planes)]
    backward = [(at, (at - 1) % planes) for at in range(planes)]

    def plane_exchange(rows):
        return lax.all_to_all(rows, PLANE, split_axis=0, concat_axis=0, tiled=True)

    weight_in = pltpu.with_memory_space_constraint(expert_in, pltpu.HBM)
    weight_out = pltpu.with_memory_space_constraint(expert_out, pltpu.HBM)

    def pass_on(rows, perm):
        return lax.ppermute(rows, "z", perm)

    rising, falling = [own], [own]
    for _ in range(3):
        rising.append(pass_on(rising[-1], forward))
        falling.append(pass_on(falling[-1], backward))
    far = jnp.concatenate(
        [pass_on(rising[3][:half], forward), pass_on(falling[3][half:], backward)],
        axis=0,
    )
    picked = (
        [own, rising[1], falling[1]],
        [rising[2], falling[2]],
        [rising[3], falling[3], far],
    )
    sent = []
    for group in picked:
        rows = dispatch_rows(plane, group, width)
        sent.append(plane_exchange(rows))
    made_0, made_1, made_2 = run_expert(
        sent[:2], ((CAP, 2 * CAP), (2 * CAP,)), weight_in, weight_out
    )
    (made_3,) = run_expert(sent[2:], ((3 * CAP,),), weight_in, weight_out)
    back = [plane_exchange(rows) for rows in (made_0, made_1, made_2, made_3)]

    to_rising, to_falling = combine_far(plane, far, back[3], width)
    for step in (3, 2, 1):
        to_rising = pass_on(to_rising, backward)
        to_falling = pass_on(to_falling, forward)
        to_rising, to_falling = combine_pair(
            plane,
            (rising[step], falling[step]),
            back[step],
            (to_rising, to_falling),
            width,
        )
    to_rising = pass_on(to_rising, backward)
    to_falling = pass_on(to_falling, forward)
    return combine_last(plane, own, back[0], (to_rising, to_falling), residual_mid, width)


def solution(mesh):
    grid = Mesh(mesh.devices.reshape(8, 4, 2, 4), ("z", "y", "c", "x"))
    rows = P(("x", *SEQ), None)
    return jax.shard_map(
        local,
        mesh=grid,
        in_specs=(
            rows,
            P(),
            P(None, SEQ),
            P(),
            P(SEQ, None),
            P(),
            P(SEQ, None, None),
            P(SEQ, None, None),
            rows,
            rows,
        ),
        out_specs=rows,
        check_vma=False,
    )
```

```python
import math

import jax
import jax.numpy as jnp
from jax import lax
from jax.experimental import pallas as pl
from jax.experimental.pallas import tpu as pltpu
from jax.sharding import Mesh
from jax.sharding import PartitionSpec as P

QH = 32
KVH = 4
HD = 64
WIN = 128
TOP = 4


epsilon = 1e-05
rope_base = 150000.0
glu_slope = 1.702
SEQ = ("z", "y", "c")
PLANE = ("y", "c")
CAP = 16
META = 3 * TOP
TILE = 128
SPAN = 384
VMEM_LIMIT = 48 * 1024 * 1024


def shifted(value, axis, steps):
    count = math.prod(lax.axis_size(name) for name in axis)
    initial, last = (max(0, -steps), min(count, count - steps))
    return lax.ppermute(value, axis, [(source, source + steps) for source in range(initial, last)])


def norm_scale(values, gain):
    widened = values.astype(jnp.float32)
    mean_sq = jnp.mean(widened * widened, axis=-1, keepdims=True)
    return widened * lax.rsqrt(mean_sq + epsilon) * gain


def rotate(values, positions):
    half_width = values.shape[-1] // 2
    freq_steps = jnp.arange(half_width).astype(jnp.float32)
    inverse = jnp.exp(freq_steps * (-2.0 * math.log(rope_base) / values.shape[-1]))
    angles = positions[:, None] * inverse[None, :]
    cosine = jnp.cos(angles)[:, None, :]
    sine_term = jnp.sin(angles)[:, None, :]
    lower_half = values[..., :half_width]
    second = values[..., half_width:]
    return jnp.concatenate(
        [lower_half * cosine - second * sine_term, second * cosine + lower_half * sine_term],
        axis=-1,
    )


def band_block(queries, key_heads, value_heads, sinks, first_pos):
    count = queries.shape[0]
    groups = QH // KVH
    grouped = queries.reshape(count, KVH, groups, HD)
    scores = jnp.einsum(
        "tkgd,skd->kgts", grouped, key_heads, preferred_element_type=jnp.float32
    ) * (1.0 / math.sqrt(HD))
    query_pos = first_pos + jnp.arange(count)
    key_pos = first_pos - count + jnp.arange(2 * count)
    distance = query_pos[:, None] - key_pos[None, :]
    allowed = (distance >= 0) & (distance < WIN) & (key_pos >= 0)[None, :]
    scores = jnp.where(allowed[None, None, :, :], scores, -jnp.inf)
    sink_logit = sinks.reshape(KVH, groups, 1, 1)
    row_peak = jnp.maximum(jnp.max(scores, axis=-1, keepdims=True), sink_logit)
    raised = jnp.exp(scores - row_peak)
    totals = jnp.sum(raised, axis=-1, keepdims=True) + jnp.exp(sink_logit - row_peak)
    weights = (raised / totals).astype(jnp.bfloat16)
    mixture = jnp.einsum("kgts,skd->tkgd", weights, value_heads, preferred_element_type=jnp.float32)
    return mixture.reshape(count, QH * HD).astype(jnp.bfloat16)


def whole(count):
    return [pl.BlockSpec(memory_space=pltpu.VMEM)] * count


def local_call(body, out_shape, in_specs, scratch_shapes=()):
    outs = jax.tree.leaves(out_shape)
    return pl.pallas_call(
        body,
        out_shape=out_shape,
        in_specs=in_specs,
        out_specs=jax.tree.map(lambda _: pl.BlockSpec(memory_space=pltpu.VMEM), out_shape)
        if len(outs) > 1
        else pl.BlockSpec(memory_space=pltpu.VMEM),
        scratch_shapes=scratch_shapes,
        compiler_params=pltpu.CompilerParams(vmem_limit_bytes=VMEM_LIMIT),
    )


def slot_match(meta, first_expert, which):
    ids = meta[:, which : which + 1] - first_expert
    places = ids * float(CAP) + meta[:, TOP + which : TOP + which + 1]
    columns = lax.broadcasted_iota(jnp.int32, (meta.shape[0], 8 * CAP), 1).astype(jnp.float32)
    return columns == places


def dispatch_rows(plane, blocks, width):
    count = len(blocks)
    tokens = blocks[0].shape[0]

    def body(plane_ref, *refs):
        out_ref, share_ref = refs[-2:]
        first_expert = (plane_ref[0] * 8).astype(jnp.float32)
        for number in range(count):
            meta = refs[number][:, width : width + META].astype(jnp.float32)
            pick = jnp.zeros((tokens, 8 * CAP), jnp.float32)
            share = pick
            for which in range(TOP):
                here = slot_match(meta, first_expert, which)
                pick = jnp.where(here, 1.0, pick)
                share = jnp.where(here, meta[:, 2 * TOP + which : 2 * TOP + which + 1], share)
            share_ref[number] = share.astype(jnp.bfloat16)
            rows = lax.dot_general(
                pick.astype(jnp.bfloat16),
                refs[number][:, :width],
                (((0,), (0,)), ((), ())),
                preferred_element_type=jnp.float32,
            ).astype(jnp.bfloat16)
            out_ref[:, number * CAP : (number + 1) * CAP, :] = rows.reshape(8, CAP, width)

    return local_call(
        body,
        [
            jax.ShapeDtypeStruct((8, count * CAP, width), jnp.bfloat16),
            jax.ShapeDtypeStruct((count, tokens, 8 * CAP), jnp.bfloat16),
        ],
        [pl.BlockSpec(memory_space=pltpu.SMEM)] + whole(count),
    )(plane, *blocks)


def weigh_rows(share, rows):
    flat = rows.reshape(8 * CAP, rows.shape[-1])
    return jnp.dot(share, flat, preferred_element_type=jnp.float32)


def run_expert(groups, parts, weight_in, weight_out):
    width = groups[0].shape[-1]
    hidden = weight_out.shape[1]
    total = sum(8 * group.shape[1] for group in groups)
    tiles = total // TILE
    count_in = width // SPAN
    rest = count_in * SPAN
    shapes = [(8, size, width) for sizes in parts for size in sizes]

    def body(*refs):
        ins, (in_hbm, out_hbm) = refs[: len(groups)], refs[len(groups) : len(groups) + 2]
        outs = refs[len(groups) + 2 : len(groups) + 2 + len(shapes)]
        in_ref, out_ref, rows_ref, acc_ref, sems = refs[len(groups) + 2 + len(shapes) :]

        def fetch(low, size, sem):
            return pltpu.make_async_copy(
                in_hbm.at[0, pl.ds(low, size)], in_ref.at[pl.ds(low, size)], sems.at[sem]
            )

        last = fetch(rest, width - rest, count_in)
        last.start()
        for n in range(count_in):
            fetch(n * SPAN, SPAN, n).start()
        down = pltpu.make_async_copy(out_hbm.at[0], out_ref, sems.at[count_in + 1])
        down.start()
        start = 0
        for rows in ins:
            count = 8 * rows.shape[1]
            rows_ref[start : start + count] = rows[...].reshape(count, width)
            start += count
        last.wait()

        def first(tile, carry):
            at = pl.ds(pl.multiple_of(tile * TILE, TILE), TILE)
            acc_ref[at] = jnp.dot(
                rows_ref[at, rest:], in_ref[rest:], preferred_element_type=jnp.float32
            )
            return carry

        lax.fori_loop(0, tiles, first, 0)

        def more(n, carry):
            low = pl.multiple_of(n * SPAN, SPAN)
            fetch(low, SPAN, n).wait()

            def multiply(tile, carry):
                at = pl.ds(pl.multiple_of(tile * TILE, TILE), TILE)
                acc_ref[at] += jnp.dot(
                    rows_ref[at, pl.ds(low, SPAN)],
                    in_ref[pl.ds(low, SPAN)],
                    preferred_element_type=jnp.float32,
                )
                return carry

            return lax.fori_loop(0, tiles, multiply, carry)

        lax.fori_loop(0, count_in, more, 0)
        down.wait()

        def finish(tile, carry):
            at = pl.ds(pl.multiple_of(tile * TILE, TILE), TILE)
            gate_part = acc_ref[at, :hidden]
            up_part = acc_ref[at, hidden:]
            activated = (
                gate_part * (1.0 / (1.0 + jnp.exp(-glu_slope * gate_part))) * (up_part + 1.0)
            ).astype(jnp.bfloat16)
            rows_ref[at] = jnp.dot(
                activated, out_ref[...], preferred_element_type=jnp.float32
            ).astype(jnp.bfloat16)
            return carry

        lax.fori_loop(0, tiles, finish, 0)
        start, place = 0, 0
        for group, sizes in zip(ins, parts):
            count = 8 * group.shape[1]
            made = rows_ref[start : start + count].reshape(8, group.shape[1], width)
            at = 0
            for size in sizes:
                outs[place][...] = made[:, at : at + size]
                at += size
                place += 1
            start += count

    return pl.pallas_call(
        body,
        out_shape=[jax.ShapeDtypeStruct(shape, jnp.bfloat16) for shape in shapes],
        in_specs=whole(len(groups)) + [pl.BlockSpec(memory_space=pltpu.HBM)] * 2,
        out_specs=whole(len(shapes)),
        scratch_shapes=[
            pltpu.VMEM((width, 2 * hidden), jnp.bfloat16),
            pltpu.VMEM((hidden, width), jnp.bfloat16),
            pltpu.VMEM((total, width), jnp.bfloat16),
            pltpu.VMEM((total, 2 * hidden), jnp.float32),
            pltpu.SemaphoreType.DMA((count_in + 2,)),
        ],
        compiler_params=pltpu.CompilerParams(vmem_limit_bytes=VMEM_LIMIT),
    )(*groups, weight_in, weight_out)


def project_in(tokens, gain, gathered, depth):
    count, width = tokens.shape
    shards = gathered.shape[0]
    chunks = 4
    step = shards // chunks

    def body(tokens_ref, gain_ref, gathered_hbm, out_ref, weight_ref, sems):
        copies = [
            pltpu.make_async_copy(
                gathered_hbm.at[pl.ds(n * step, step), pl.ds(0, depth)],
                weight_ref.at[pl.ds(n * step, step)],
                sems.at[n],
            )
            for n in range(chunks)
        ]
        for copy in copies:
            copy.start()
        normed = norm_scale(tokens_ref[...], gain_ref[...]).astype(jnp.bfloat16)
        for n, copy in enumerate(copies):
            copy.wait()
            weight = weight_ref[n * step : (n + 1) * step].reshape(step * depth, width)
            out_ref[:, n * step * depth : (n + 1) * step * depth] = lax.dot_general(
                normed, weight, (((1,), (1,)), ((), ())), preferred_element_type=jnp.float32
            )

    return pl.pallas_call(
        body,
        out_shape=jax.ShapeDtypeStruct((count, shards * depth), jnp.float32),
        in_specs=whole(2) + [pl.BlockSpec(memory_space=pltpu.HBM)],
        out_specs=pl.BlockSpec(memory_space=pltpu.VMEM),
        scratch_shapes=[
            pltpu.VMEM((shards, depth, width), jnp.bfloat16),
            pltpu.SemaphoreType.DMA((chunks,)),
        ],
        compiler_params=pltpu.CompilerParams(vmem_limit_bytes=VMEM_LIMIT),
    )(tokens, gain.reshape(1, width), gathered)


def project_out(attention, gathered, skip, tokens, gain, columns):
    count, width = tokens.shape
    shards, depth = gathered.shape[0], gathered.shape[1] - skip
    chunks = 4
    step = shards // chunks

    def body(attention_ref, gathered_hbm, tokens_ref, gain_ref, columns_ref, *refs):
        residual_ref, own_ref, weight_ref, sems = refs
        copies = [
            pltpu.make_async_copy(
                gathered_hbm.at[pl.ds(n * step, step), pl.ds(skip, depth)],
                weight_ref.at[pl.ds(n * step, step)],
                sems.at[n],
            )
            for n in range(chunks)
        ]
        for copy in copies:
            copy.start()
        total = tokens_ref[...].astype(jnp.float32)
        for n, copy in enumerate(copies):
            copy.wait()
            total += jnp.dot(
                attention_ref[:, n * step * depth : (n + 1) * step * depth],
                weight_ref[n * step : (n + 1) * step].reshape(step * depth, width),
                preferred_element_type=jnp.float32,
            )
        middle = total.astype(jnp.bfloat16)
        residual_ref[...] = middle
        own_ref[:, :width] = norm_scale(middle, gain_ref[...]).astype(jnp.bfloat16)
        own_ref[:, width:] = columns_ref[...]

    return pl.pallas_call(
        body,
        out_shape=[
            jax.ShapeDtypeStruct((count, width), jnp.bfloat16),
            jax.ShapeDtypeStruct((count, width + columns.shape[1]), jnp.bfloat16),
        ],
        in_specs=whole(1) + [pl.BlockSpec(memory_space=pltpu.HBM)] + whole(3),
        out_specs=whole(2),
        scratch_shapes=[
            pltpu.VMEM((shards, depth, width), jnp.bfloat16),
            pltpu.SemaphoreType.DMA((chunks,)),
        ],
        compiler_params=pltpu.CompilerParams(vmem_limit_bytes=VMEM_LIMIT),
    )(attention, gathered, tokens, gain.reshape(1, width), columns)


def combine_far(shares, rows):
    last, count = shares.shape[0] - 1, shares.shape[1]
    half, width = count // 2, rows.shape[-1]

    def body(share_ref, rows_ref, low_ref, high_ref):
        summed = weigh_rows(share_ref[last], rows_ref[:, last * CAP : (last + 1) * CAP, :])
        low_ref[...] = summed[:half].astype(jnp.bfloat16)
        high_ref[...] = summed[half:].astype(jnp.bfloat16)

    return local_call(
        body, [jax.ShapeDtypeStruct((half, width), jnp.bfloat16)] * 2, whole(2)
    )(shares, rows)


def combine_pair(shares, first, rows, arrived):
    count, width = shares.shape[1], rows.shape[-1]

    def body(share_ref, rows_ref, rising_ref, falling_ref, *outs):
        for number, came in enumerate((rising_ref, falling_ref)):
            summed = weigh_rows(
                share_ref[first + number], rows_ref[:, number * CAP : (number + 1) * CAP, :]
            )
            size = came.shape[0]
            if size == count:
                outs[number][...] = (summed + came[...].astype(jnp.float32)).astype(jnp.bfloat16)
            else:
                at = number * size
                other = size - at
                outs[number][at : at + size] = (
                    summed[at : at + size] + came[...].astype(jnp.float32)
                ).astype(jnp.bfloat16)
                outs[number][other : other + size] = summed[other : other + size].astype(
                    jnp.bfloat16
                )

    return local_call(
        body, [jax.ShapeDtypeStruct((count, width), jnp.bfloat16)] * 2, whole(4)
    )(shares, rows, *arrived)


def combine_last(shares, rows, arrived, residual_mid):
    def body(share_ref, rows_ref, rising_ref, falling_ref, residual_ref, out_ref):
        out_ref[...] = (
            residual_ref[...].astype(jnp.float32)
            + weigh_rows(share_ref[0], rows_ref[...])
            + rising_ref[...].astype(jnp.float32)
            + falling_ref[...].astype(jnp.float32)
        ).astype(jnp.bfloat16)

    return local_call(
        body, jax.ShapeDtypeStruct(residual_mid.shape, jnp.bfloat16), whole(5)
    )(shares, rows, *arrived, residual_mid)


def routing_columns(expert_ids, gate_ints, experts):
    rows = expert_ids.shape[0]
    flat_ids = expert_ids.reshape(-1)
    onehot = (flat_ids[:, None] == jnp.arange(experts)[None, :]).astype(jnp.int32)
    before = jnp.cumsum(onehot, axis=0) - onehot
    slot_index = jnp.sum(before * onehot, axis=1).reshape(rows, TOP)
    route_weight = gate_ints.astype(jnp.float32)
    route_weight = route_weight / jnp.sum(route_weight, axis=-1, keepdims=True)
    return jnp.concatenate(
        [expert_ids.astype(jnp.float32), slot_index.astype(jnp.float32), route_weight], axis=1
    ).astype(jnp.bfloat16)


def local(
    tokens,
    norm_gain,
    qkv_weight,
    sinks,
    out_weight,
    moe_gain,
    expert_in,
    expert_out,
    expert_ids,
    gate_ints,
):
    local_rows = tokens.shape[0]
    width = tokens.shape[1]
    devices = math.prod(lax.axis_size(name) for name in SEQ)
    device_index = lax.axis_index(SEQ)
    query_cols = QH * HD
    key_cols = KVH * HD
    qkv_part = qkv_weight.shape[1]

    both = jnp.concatenate([qkv_weight.T, out_weight], axis=0)
    gathered = lax.all_gather(both, SEQ, axis=0)
    projections = project_in(tokens, norm_gain, gathered, qkv_part)
    first_pos = device_index * local_rows
    positions = (first_pos + jnp.arange(local_rows)).astype(jnp.float32)
    queries = rotate(projections[:, :query_cols].reshape(local_rows, QH, HD), positions).astype(
        jnp.bfloat16
    )
    key_heads = rotate(
        projections[:, query_cols : query_cols + key_cols].reshape(local_rows, KVH, HD), positions
    ).astype(jnp.bfloat16)
    value_heads = (
        projections[:, query_cols + key_cols :].reshape(local_rows, KVH, HD).astype(jnp.bfloat16)
    )
    prev_keys, prev_values = shifted((key_heads, value_heads), SEQ, 1)
    key_block = jnp.concatenate([prev_keys, key_heads], axis=0)
    value_block = jnp.concatenate([prev_values, value_heads], axis=0)
    attention = band_block(queries, key_block, value_block, sinks, first_pos)
    columns = routing_columns(expert_ids, gate_ints, devices)
    residual_mid, own = project_out(
        attention,
        gathered,
        qkv_part,
        tokens,
        moe_gain,
        columns,
    )

    planes = lax.axis_size("z")
    half = local_rows // 2
    plane = lax.axis_index("z").astype(jnp.int32).reshape(1)
    forward = [(at, (at + 1) % planes) for at in range(planes)]
    backward = [(at, (at - 1) % planes) for at in range(planes)]

    def plane_exchange(rows):
        return lax.all_to_all(rows, PLANE, split_axis=0, concat_axis=0, tiled=True)

    weight_in = pltpu.with_memory_space_constraint(expert_in, pltpu.HBM)
    weight_out = pltpu.with_memory_space_constraint(expert_out, pltpu.HBM)

    def pass_on(rows, perm):
        return lax.ppermute(rows, "z", perm)

    rising, falling = [own], [own]
    for _ in range(3):
        rising.append(pass_on(rising[-1], forward))
        falling.append(pass_on(falling[-1], backward))
    far = jnp.concatenate(
        [pass_on(rising[3][:half], forward), pass_on(falling[3][half:], backward)],
        axis=0,
    )
    picked = (
        [own, rising[1], falling[1]],
        [rising[2], falling[2]],
        [rising[3], falling[3], far],
    )
    sent, shares = [], []
    for group in picked:
        rows, share = dispatch_rows(plane, group, width)
        shares.append(share)
        sent.append(plane_exchange(rows))
    made_0, made_1, made_2 = run_expert(
        sent[:2], ((CAP, 2 * CAP), (2 * CAP,)), weight_in, weight_out
    )
    (made_3,) = run_expert(sent[2:], ((3 * CAP,),), weight_in, weight_out)
    back = [plane_exchange(rows) for rows in (made_0, made_1, made_2, made_3)]

    to_rising, to_falling = combine_far(shares[2], back[3])
    for step in (3, 2, 1):
        to_rising = pass_on(to_rising, backward)
        to_falling = pass_on(to_falling, forward)
        to_rising, to_falling = combine_pair(
            shares[step - 1], int(step == 1), back[step], (to_rising, to_falling)
        )
    to_rising = pass_on(to_rising, backward)
    to_falling = pass_on(to_falling, forward)
    return combine_last(shares[0], back[0], (to_rising, to_falling), residual_mid)


def solution(mesh):
    grid = Mesh(mesh.devices.reshape(8, 4, 2, 4), ("z", "y", "c", "x"))
    rows = P(("x", *SEQ), None)
    return jax.shard_map(
        local,
        mesh=grid,
        in_specs=(
            rows,
            P(),
            P(None, SEQ),
            P(),
            P(SEQ, None),
            P(),
            P(SEQ, None, None),
            P(SEQ, None, None),
            rows,
            rows,
        ),
        out_specs=rows,
        check_vma=False,
    )
```

```python
import math

import jax
import jax.numpy as jnp
from jax import lax
from jax.experimental import pallas as pl
from jax.experimental.pallas import tpu as pltpu
from jax.sharding import Mesh
from jax.sharding import PartitionSpec as P

QH = 32
KVH = 4
HD = 64
WIN = 128
TOP = 4


epsilon = 1e-05
rope_base = 150000.0
glu_slope = 1.702
SEQ = ("z", "y", "c")
PLANE = ("y", "c")
CAP = 16
META = 3 * TOP
TILE = 128
SPAN = 384
VMEM_LIMIT = 48 * 1024 * 1024


def shifted(value, axis, steps):
    count = math.prod(lax.axis_size(name) for name in axis)
    initial, last = (max(0, -steps), min(count, count - steps))
    return lax.ppermute(value, axis, [(source, source + steps) for source in range(initial, last)])


def norm_scale(values, gain):
    widened = values.astype(jnp.float32)
    mean_sq = jnp.mean(widened * widened, axis=-1, keepdims=True)
    return widened * lax.rsqrt(mean_sq + epsilon) * gain


def rotate(values, positions):
    half_width = values.shape[-1] // 2
    freq_steps = jnp.arange(half_width).astype(jnp.float32)
    inverse = jnp.exp(freq_steps * (-2.0 * math.log(rope_base) / values.shape[-1]))
    angles = positions[:, None] * inverse[None, :]
    cosine = jnp.cos(angles)[:, None, :]
    sine_term = jnp.sin(angles)[:, None, :]
    lower_half = values[..., :half_width]
    second = values[..., half_width:]
    return jnp.concatenate(
        [lower_half * cosine - second * sine_term, second * cosine + lower_half * sine_term],
        axis=-1,
    )


def band_block(queries, key_heads, value_heads, sinks, first_pos):
    count = queries.shape[0]
    groups = QH // KVH
    grouped = queries.reshape(count, KVH, groups, HD)
    scores = jnp.einsum(
        "tkgd,skd->kgts", grouped, key_heads, preferred_element_type=jnp.float32
    ) * (1.0 / math.sqrt(HD))
    query_pos = first_pos + jnp.arange(count)
    key_pos = first_pos - count + jnp.arange(2 * count)
    distance = query_pos[:, None] - key_pos[None, :]
    allowed = (distance >= 0) & (distance < WIN) & (key_pos >= 0)[None, :]
    scores = jnp.where(allowed[None, None, :, :], scores, -jnp.inf)
    sink_logit = sinks.reshape(KVH, groups, 1, 1)
    row_peak = jnp.maximum(jnp.max(scores, axis=-1, keepdims=True), sink_logit)
    raised = jnp.exp(scores - row_peak)
    totals = jnp.sum(raised, axis=-1, keepdims=True) + jnp.exp(sink_logit - row_peak)
    weights = (raised / totals).astype(jnp.bfloat16)
    mixture = jnp.einsum("kgts,skd->tkgd", weights, value_heads, preferred_element_type=jnp.float32)
    return mixture.reshape(count, QH * HD).astype(jnp.bfloat16)


def whole(count):
    return [pl.BlockSpec(memory_space=pltpu.VMEM)] * count


def local_call(body, out_shape, in_specs, scratch_shapes=()):
    outs = jax.tree.leaves(out_shape)
    return pl.pallas_call(
        body,
        out_shape=out_shape,
        in_specs=in_specs,
        out_specs=jax.tree.map(lambda _: pl.BlockSpec(memory_space=pltpu.VMEM), out_shape)
        if len(outs) > 1
        else pl.BlockSpec(memory_space=pltpu.VMEM),
        scratch_shapes=scratch_shapes,
        compiler_params=pltpu.CompilerParams(vmem_limit_bytes=VMEM_LIMIT),
    )


def slot_match(meta, first_expert, which):
    ids = meta[:, which : which + 1] - first_expert
    places = ids * float(CAP) + meta[:, TOP + which : TOP + which + 1]
    columns = lax.broadcasted_iota(jnp.int32, (meta.shape[0], 8 * CAP), 1).astype(jnp.float32)
    return columns == places


def dispatch_rows(plane, blocks, width):
    count = len(blocks)
    tokens = blocks[0].shape[0]

    def body(plane_ref, *refs):
        out_ref, share_ref = refs[-2:]
        first_expert = (plane_ref[0] * 8).astype(jnp.float32)
        for number in range(count):
            meta = refs[number][:, width : width + META].astype(jnp.float32)
            pick = jnp.zeros((tokens, 8 * CAP), jnp.float32)
            share = pick
            for which in range(TOP):
                here = slot_match(meta, first_expert, which)
                pick = jnp.where(here, 1.0, pick)
                share = jnp.where(here, meta[:, 2 * TOP + which : 2 * TOP + which + 1], share)
            share_ref[number] = share.astype(jnp.bfloat16)
            rows = lax.dot_general(
                pick.astype(jnp.bfloat16),
                refs[number][:, :width],
                (((0,), (0,)), ((), ())),
                preferred_element_type=jnp.float32,
            ).astype(jnp.bfloat16)
            out_ref[:, number * CAP : (number + 1) * CAP, :] = rows.reshape(8, CAP, width)

    return local_call(
        body,
        [
            jax.ShapeDtypeStruct((8, count * CAP, width), jnp.bfloat16),
            jax.ShapeDtypeStruct((count, tokens, 8 * CAP), jnp.bfloat16),
        ],
        [pl.BlockSpec(memory_space=pltpu.SMEM)] + whole(count),
    )(plane, *blocks)


def weigh_rows(share, rows):
    flat = rows.reshape(8 * CAP, rows.shape[-1])
    return jnp.dot(share, flat, preferred_element_type=jnp.float32)


def run_expert(groups, parts, weight_in, weight_out):
    width = groups[0].shape[-1]
    hidden = weight_out.shape[1]
    total = sum(8 * group.shape[1] for group in groups)
    tiles = total // TILE
    count_in = width // SPAN
    rest = count_in * SPAN
    shapes = [(8, size, width) for sizes in parts for size in sizes]

    def body(*refs):
        ins, (in_hbm, out_hbm) = refs[: len(groups)], refs[len(groups) : len(groups) + 2]
        outs = refs[len(groups) + 2 : len(groups) + 2 + len(shapes)]
        in_ref, out_ref, rows_ref, acc_ref, sems = refs[len(groups) + 2 + len(shapes) :]

        def fetch(low, size, sem):
            return pltpu.make_async_copy(
                in_hbm.at[0, pl.ds(low, size)], in_ref.at[pl.ds(low, size)], sems.at[sem]
            )

        last = fetch(rest, width - rest, count_in)
        last.start()
        for n in range(count_in):
            fetch(n * SPAN, SPAN, n).start()
        down = pltpu.make_async_copy(out_hbm.at[0], out_ref, sems.at[count_in + 1])
        down.start()
        start = 0
        for rows in ins:
            count = 8 * rows.shape[1]
            rows_ref[start : start + count] = rows[...].reshape(count, width)
            start += count
        last.wait()

        def first(tile, carry):
            at = pl.ds(pl.multiple_of(tile * TILE, TILE), TILE)
            acc_ref[at] = jnp.dot(
                rows_ref[at, rest:], in_ref[rest:], preferred_element_type=jnp.float32
            )
            return carry

        lax.fori_loop(0, tiles, first, 0)

        def more(n, carry):
            low = pl.multiple_of(n * SPAN, SPAN)
            fetch(low, SPAN, n).wait()

            def multiply(tile, carry):
                at = pl.ds(pl.multiple_of(tile * TILE, TILE), TILE)
                acc_ref[at] += jnp.dot(
                    rows_ref[at, pl.ds(low, SPAN)],
                    in_ref[pl.ds(low, SPAN)],
                    preferred_element_type=jnp.float32,
                )
                return carry

            return lax.fori_loop(0, tiles, multiply, carry)

        lax.fori_loop(0, count_in, more, 0)
        down.wait()

        def finish(tile, carry):
            at = pl.ds(pl.multiple_of(tile * TILE, TILE), TILE)
            gate_part = acc_ref[at, :hidden]
            up_part = acc_ref[at, hidden:]
            activated = (
                gate_part * (1.0 / (1.0 + jnp.exp(-glu_slope * gate_part))) * (up_part + 1.0)
            ).astype(jnp.bfloat16)
            rows_ref[at] = jnp.dot(
                activated, out_ref[...], preferred_element_type=jnp.float32
            ).astype(jnp.bfloat16)
            return carry

        lax.fori_loop(0, tiles, finish, 0)
        start, place = 0, 0
        for group, sizes in zip(ins, parts):
            count = 8 * group.shape[1]
            made = rows_ref[start : start + count].reshape(8, group.shape[1], width)
            at = 0
            for size in sizes:
                outs[place][...] = made[:, at : at + size]
                at += size
                place += 1
            start += count

    return pl.pallas_call(
        body,
        out_shape=[jax.ShapeDtypeStruct(shape, jnp.bfloat16) for shape in shapes],
        in_specs=whole(len(groups)) + [pl.BlockSpec(memory_space=pltpu.HBM)] * 2,
        out_specs=whole(len(shapes)),
        scratch_shapes=[
            pltpu.VMEM((width, 2 * hidden), jnp.bfloat16),
            pltpu.VMEM((hidden, width), jnp.bfloat16),
            pltpu.VMEM((total, width), jnp.bfloat16),
            pltpu.VMEM((total, 2 * hidden), jnp.float32),
            pltpu.SemaphoreType.DMA((count_in + 2,)),
        ],
        compiler_params=pltpu.CompilerParams(vmem_limit_bytes=VMEM_LIMIT),
    )(*groups, weight_in, weight_out)


def project_in(tokens, gain, gathered, depth):
    count, width = tokens.shape
    shards = gathered.shape[0]
    chunks = 4
    step = shards // chunks

    def body(tokens_ref, gain_ref, gathered_hbm, out_ref, weight_ref, sems):
        copies = [
            pltpu.make_async_copy(
                gathered_hbm.at[pl.ds(n * step, step), pl.ds(0, depth)],
                weight_ref.at[pl.ds(n * step, step)],
                sems.at[n],
            )
            for n in range(chunks)
        ]
        for copy in copies:
            copy.start()
        normed = norm_scale(tokens_ref[...], gain_ref[...]).astype(jnp.bfloat16)
        for n, copy in enumerate(copies):
            copy.wait()
            weight = weight_ref[n * step : (n + 1) * step].reshape(step * depth, width)
            out_ref[:, n * step * depth : (n + 1) * step * depth] = lax.dot_general(
                normed, weight, (((1,), (1,)), ((), ())), preferred_element_type=jnp.float32
            )

    return pl.pallas_call(
        body,
        out_shape=jax.ShapeDtypeStruct((count, shards * depth), jnp.float32),
        in_specs=whole(2) + [pl.BlockSpec(memory_space=pltpu.HBM)],
        out_specs=pl.BlockSpec(memory_space=pltpu.VMEM),
        scratch_shapes=[
            pltpu.VMEM((shards, depth, width), jnp.bfloat16),
            pltpu.SemaphoreType.DMA((chunks,)),
        ],
        compiler_params=pltpu.CompilerParams(vmem_limit_bytes=VMEM_LIMIT),
    )(tokens, gain.reshape(1, width), gathered)


def project_out(attention, gathered, skip, tokens, gain, columns):
    count, width = tokens.shape
    shards, depth = gathered.shape[0], gathered.shape[1] - skip
    chunks = 4
    step = shards // chunks

    def body(attention_ref, gathered_hbm, tokens_ref, gain_ref, columns_ref, *refs):
        residual_ref, own_ref, weight_ref, sems = refs
        copies = [
            pltpu.make_async_copy(
                gathered_hbm.at[pl.ds(n * step, step), pl.ds(skip, depth)],
                weight_ref.at[pl.ds(n * step, step)],
                sems.at[n],
            )
            for n in range(chunks)
        ]
        for copy in copies:
            copy.start()
        total = tokens_ref[...].astype(jnp.float32)
        for n, copy in enumerate(copies):
            copy.wait()
            total += jnp.dot(
                attention_ref[:, n * step * depth : (n + 1) * step * depth],
                weight_ref[n * step : (n + 1) * step].reshape(step * depth, width),
                preferred_element_type=jnp.float32,
            )
        middle = total.astype(jnp.bfloat16)
        residual_ref[...] = middle
        own_ref[:, :width] = norm_scale(middle, gain_ref[...]).astype(jnp.bfloat16)
        own_ref[:, width:] = columns_ref[...]

    return pl.pallas_call(
        body,
        out_shape=[
            jax.ShapeDtypeStruct((count, width), jnp.bfloat16),
            jax.ShapeDtypeStruct((count, width + columns.shape[1]), jnp.bfloat16),
        ],
        in_specs=whole(1) + [pl.BlockSpec(memory_space=pltpu.HBM)] + whole(3),
        out_specs=whole(2),
        scratch_shapes=[
            pltpu.VMEM((shards, depth, width), jnp.bfloat16),
            pltpu.SemaphoreType.DMA((chunks,)),
        ],
        compiler_params=pltpu.CompilerParams(vmem_limit_bytes=VMEM_LIMIT),
    )(attention, gathered, tokens, gain.reshape(1, width), columns)


def combine_far(shares, rows):
    last, count = shares.shape[0] - 1, shares.shape[1]
    half, width = count // 2, rows.shape[-1]

    def body(share_ref, rows_ref, low_ref, high_ref):
        summed = weigh_rows(share_ref[last], rows_ref[:, last * CAP : (last + 1) * CAP, :])
        low_ref[...] = summed[:half].astype(jnp.bfloat16)
        high_ref[...] = summed[half:].astype(jnp.bfloat16)

    return local_call(
        body, [jax.ShapeDtypeStruct((half, width), jnp.bfloat16)] * 2, whole(2)
    )(shares, rows)


def combine_pair(shares, rows, arrived):
    count, width = shares.shape[1], rows.shape[-1]

    def body(share_ref, rows_ref, rising_ref, falling_ref, *outs):
        for number, came in enumerate((rising_ref, falling_ref)):
            summed = weigh_rows(
                share_ref[number], rows_ref[:, number * CAP : (number + 1) * CAP, :]
            )
            size = came.shape[0]
            if size == count:
                outs[number][...] = (summed + came[...].astype(jnp.float32)).astype(jnp.bfloat16)
            else:
                at = number * size
                other = size - at
                outs[number][at : at + size] = (
                    summed[at : at + size] + came[...].astype(jnp.float32)
                ).astype(jnp.bfloat16)
                outs[number][other : other + size] = summed[other : other + size].astype(
                    jnp.bfloat16
                )

    return local_call(
        body, [jax.ShapeDtypeStruct((count, width), jnp.bfloat16)] * 2, whole(4)
    )(shares, rows, *arrived)


def combine_last(shares, rows, arrived, residual_mid):
    def body(share_ref, rows_ref, rising_ref, falling_ref, residual_ref, out_ref):
        out_ref[...] = (
            residual_ref[...].astype(jnp.float32)
            + weigh_rows(share_ref[0], rows_ref[...])
            + rising_ref[...].astype(jnp.float32)
            + falling_ref[...].astype(jnp.float32)
        ).astype(jnp.bfloat16)

    return local_call(
        body, jax.ShapeDtypeStruct(residual_mid.shape, jnp.bfloat16), whole(5)
    )(shares, rows, *arrived, residual_mid)


def routing_columns(expert_ids, gate_ints, experts):
    rows = expert_ids.shape[0]
    flat_ids = expert_ids.reshape(-1)
    onehot = (flat_ids[:, None] == jnp.arange(experts)[None, :]).astype(jnp.int32)
    before = jnp.cumsum(onehot, axis=0) - onehot
    slot_index = jnp.sum(before * onehot, axis=1).reshape(rows, TOP)
    route_weight = gate_ints.astype(jnp.float32)
    route_weight = route_weight / jnp.sum(route_weight, axis=-1, keepdims=True)
    return jnp.concatenate(
        [expert_ids.astype(jnp.float32), slot_index.astype(jnp.float32), route_weight], axis=1
    ).astype(jnp.bfloat16)


def local(
    tokens,
    norm_gain,
    qkv_weight,
    sinks,
    out_weight,
    moe_gain,
    expert_in,
    expert_out,
    expert_ids,
    gate_ints,
):
    local_rows = tokens.shape[0]
    width = tokens.shape[1]
    devices = math.prod(lax.axis_size(name) for name in SEQ)
    device_index = lax.axis_index(SEQ)
    query_cols = QH * HD
    key_cols = KVH * HD
    qkv_part = qkv_weight.shape[1]

    both = jnp.concatenate([qkv_weight.T, out_weight], axis=0)
    gathered = lax.all_gather(both, SEQ, axis=0)
    projections = project_in(tokens, norm_gain, gathered, qkv_part)
    first_pos = device_index * local_rows
    positions = (first_pos + jnp.arange(local_rows)).astype(jnp.float32)
    queries = rotate(projections[:, :query_cols].reshape(local_rows, QH, HD), positions).astype(
        jnp.bfloat16
    )
    key_heads = rotate(
        projections[:, query_cols : query_cols + key_cols].reshape(local_rows, KVH, HD), positions
    ).astype(jnp.bfloat16)
    value_heads = (
        projections[:, query_cols + key_cols :].reshape(local_rows, KVH, HD).astype(jnp.bfloat16)
    )
    prev_keys, prev_values = shifted((key_heads, value_heads), SEQ, 1)
    key_block = jnp.concatenate([prev_keys, key_heads], axis=0)
    value_block = jnp.concatenate([prev_values, value_heads], axis=0)
    attention = band_block(queries, key_block, value_block, sinks, first_pos)
    columns = routing_columns(expert_ids, gate_ints, devices)
    residual_mid, own = project_out(
        attention,
        gathered,
        qkv_part,
        tokens,
        moe_gain,
        columns,
    )

    planes = lax.axis_size("z")
    half = local_rows // 2
    plane = lax.axis_index("z").astype(jnp.int32).reshape(1)
    forward = [(at, (at + 1) % planes) for at in range(planes)]
    backward = [(at, (at - 1) % planes) for at in range(planes)]

    def plane_exchange(rows):
        return lax.all_to_all(rows, PLANE, split_axis=0, concat_axis=0, tiled=True)

    weight_in = pltpu.with_memory_space_constraint(expert_in, pltpu.HBM)
    weight_out = pltpu.with_memory_space_constraint(expert_out, pltpu.HBM)

    def pass_on(rows, perm):
        return lax.ppermute(rows, "z", perm)

    rising, falling = [own], [own]
    for _ in range(3):
        rising.append(pass_on(rising[-1], forward))
        falling.append(pass_on(falling[-1], backward))
    far = jnp.concatenate(
        [pass_on(rising[3][:half], forward), pass_on(falling[3][half:], backward)],
        axis=0,
    )
    picked = (
        [own],
        [rising[1], falling[1]],
        [rising[2], falling[2]],
        [rising[3], falling[3], far],
    )
    sent, shares = [], []
    for group in picked:
        rows, share = dispatch_rows(plane, group, width)
        shares.append(share)
        sent.append(plane_exchange(rows))
    made_0, made_1, made_2 = run_expert(
        sent[:3], ((CAP,), (2 * CAP,), (2 * CAP,)), weight_in, weight_out
    )
    (made_3,) = run_expert(sent[3:], ((3 * CAP,),), weight_in, weight_out)
    back = [plane_exchange(rows) for rows in (made_0, made_1, made_2, made_3)]

    to_rising, to_falling = combine_far(shares[3], back[3])
    for step in (3, 2, 1):
        to_rising = pass_on(to_rising, backward)
        to_falling = pass_on(to_falling, forward)
        to_rising, to_falling = combine_pair(
            shares[step], back[step], (to_rising, to_falling)
        )
    to_rising = pass_on(to_rising, backward)
    to_falling = pass_on(to_falling, forward)
    return combine_last(shares[0], back[0], (to_rising, to_falling), residual_mid)


def solution(mesh):
    grid = Mesh(mesh.devices.reshape(8, 4, 2, 4), ("z", "y", "c", "x"))
    rows = P(("x", *SEQ), None)
    return jax.shard_map(
        local,
        mesh=grid,
        in_specs=(
            rows,
            P(),
            P(None, SEQ),
            P(),
            P(SEQ, None),
            P(),
            P(SEQ, None, None),
            P(SEQ, None, None),
            rows,
            rows,
        ),
        out_specs=rows,
        check_vma=False,
    )
```
